512 devices in a mesh: ops: 32 (over x, z), sec: 16 (over y, core).
Axes of the slice: x: 4, y: 8, z: 8, core: 2. Of those that a mesh axis runs over, the one named last changes fastest.
Arguments:
- sector_states: int32 [16], P('sec'), may hold values from 85 to 256, as said below
- psi_guess: bfloat16 [16, 256, 256], P('sec'), may hold values from -6 to 6
- precond_diag: bfloat16 [16, 256, 256], P('sec'), may hold values from -12 to 12
- left_ops: float32 [64, 16, 256, 256], P('ops', 'sec'), may hold values from -0.375 to 0.375
- right_ops: float32 [64, 16, 256, 256], P('ops', 'sec'), may hold values from -0.375 to 0.375
- couple: int32 [64, 16], P('ops', 'sec'), may hold values from -1 to 15, as said below
- new_sector: int32 [16], P('sec'), may hold values from 0 to 15, as said below
Outputs:
- wavefunction: float32 [16, 256, 256], P('sec')
- rotated_ops: float32 [64, 16, 256, 256], P('ops', 'sec')
The draws below stay inside these ranges and needn't reach their ends.
Inputs may be any that keep to these rules, and one draw needn't show every extreme that they name: `sector_states`: at least one sector has 256 states. couple[p, s] is s - 1, s or s + 1, or -1 where that lies outside the sectors. `new_sector`: each aligned pair of sectors 2k, 2k + 1 either keeps its labels or swaps them; the pair with 2k = 8 always swaps.
All inputs are finite; a program needn't handle non-finite values.
Results may differ from the reference program's by a relative error of at most 0.0003.
Values sent between devices are 32-bit elements; how exact they have to be, the bound alone decides.
A program may use at most 64 MiB of HBM per device.

```python
import jax
import jax.numpy as jnp
from jax import lax

MAXS = 256
UPDATES = 2
PAIRS = 64
NSEC = 16


def draw_sector_states(key, part):
    states = jax.random.randint(key, (NSEC,), MAXS // 3, MAXS + 1)
    where = jax.random.randint(jax.random.fold_in(key, 7), (), 0, NSEC)
    return states.at[where].set(MAXS).astype(jnp.int32)


def draw_couple(key, part):
    offset = jax.random.randint(key, (PAIRS, NSEC), -1, 2)
    sector = jnp.arange(NSEC, dtype=jnp.int32)[None, :]
    source = sector + offset
    outside = (source < 0) | (source >= NSEC)
    return jnp.where(outside, -1, source).astype(jnp.int32)


def draw_new_sector(key, part):
    flips = jax.random.randint(key, (NSEC // 2,), 0, 2)
    flips = flips.at[NSEC // 4].set(1)
    base = 2 * jnp.arange(NSEC // 2, dtype=jnp.int32)
    labels = jnp.stack([base + flips, base + 1 - flips], axis=1)
    return labels.reshape(NSEC).astype(jnp.int32)


def levels(stream_key, extent, cuts, low, largest):
    def one(position, parts):
        steps = jax.random.uniform(jax.random.fold_in(jax.random.fold_in(stream_key, 6), position), (parts,), jnp.float32, low / len(cuts), largest / len(cuts))
        return jnp.repeat(jnp.exp(steps), extent[position] // parts).reshape((-1,) + (1,) * (len(extent) - position - 1))

    loudness = one(*cuts[0])
    for cut in cuts[1:]:
        loudness = loudness * one(*cut)
    return loudness


def centred(own_key, dims, width, limit, pieces=(), kind=jnp.bfloat16):
    drawn = jax.random.normal(own_key, dims, jnp.float32) * width
    if len(pieces) > 0:
        drawn = levels(own_key, dims, pieces, -0.22, 0.18) * drawn
    return jnp.clip(drawn, min=-limit, max=limit).astype(kind)


def setup_inputs(seed: int = 0) -> dict:
    seeds = jax.random.split(jax.random.key(seed), 8)
    return {
        "sector_states": draw_sector_states(jax.random.fold_in(seeds[7], 71), 0),
        "psi_guess": centred(seeds[1], (NSEC, MAXS, MAXS), 1.0, 6.0, ((0, 16),)),
        "precond_diag": centred(seeds[2], (NSEC, MAXS, MAXS), 2.0, 12.0, ((0, 16),)),
        "left_ops": centred(seeds[3], (PAIRS, NSEC, MAXS, MAXS), MAXS ** -0.5, 0.375, ((0, 32), (1, 16)), jnp.float32),
        "right_ops": centred(seeds[4], (PAIRS, NSEC, MAXS, MAXS), MAXS ** -0.5, 0.375, ((0, 32), (1, 16)), jnp.float32),
        "couple": draw_couple(jax.random.fold_in(seeds[7], 71), 0),
        "new_sector": draw_new_sector(jax.random.fold_in(seeds[7], 71), 0),
    }


HIGH = lax.Precision.HIGHEST

def apply_ham(vec, left_ops, right_ops, couple, live):

    def step(total, item):
        left, right, source = item
        valid = (source >= 0).astype(jnp.float32)
        picked = vec[jnp.clip(source, 0, NSEC - 1)] * valid[:, None, None]
        mixed = jnp.einsum('sij,sjk->sik', left, picked, precision=HIGH)
        return (total + jnp.einsum('sik,slk->sil', mixed, right, precision=HIGH), None)
    total, _ = lax.scan(step, jnp.zeros(vec.shape, jnp.float32), (left_ops, right_ops, couple))
    return total * live

def reference(sector_states, psi_guess, precond_diag, left_ops, right_ops, couple, new_sector):
    index = jnp.arange(MAXS, dtype=jnp.int32)
    sizes = sector_states[:, None, None]
    live = ((index[None, :, None] < sizes) & (index[None, None, :] < sizes)).astype(jnp.float32)
    diag = precond_diag.astype(jnp.float32)
    vecx = psi_guess.astype(jnp.float32) * live
    vecx = vecx * lax.rsqrt(jnp.sum(vecx * vecx) + 1e-06)
    hvec = apply_ham(vecx, left_ops, right_ops, couple, live)
    theta = jnp.sum(vecx * hvec)
    for update in range(UPDATES):
        corr = live * (hvec - theta * vecx) / (jnp.abs(diag - theta) + 1.0)
        corr = corr - jnp.sum(vecx * corr) * vecx
        corr = corr * lax.rsqrt(jnp.sum(corr * corr) + 1e-06)
        hcorr = apply_ham(corr, left_ops, right_ops, couple, live)
        first = theta
        middle = 0.5 * (jnp.sum(vecx * hcorr) + jnp.sum(corr * hvec))
        last = jnp.sum(corr * hcorr)
        angle = 0.5 * jnp.arctan2(-2.0 * middle, last - first)
        vecx = jnp.cos(angle) * vecx + jnp.sin(angle) * corr
        hvec = jnp.cos(angle) * hvec + jnp.sin(angle) * hcorr
        theta = 0.5 * (first + last) - 0.5 * jnp.sqrt((last - first) ** 2 + 4.0 * middle * middle)
    wavefunction = vecx * jnp.sqrt(jnp.float32(NSEC * MAXS * MAXS))
    valid = (couple >= 0).astype(jnp.float32)
    picked = wavefunction[jnp.clip(couple, 0, NSEC - 1)] * valid[:, :, None, None]
    inner = jnp.einsum('psjk,pskl->psjl', left_ops, picked, precision=HIGH)
    turned = jnp.einsum('sji,psjl->psil', wavefunction, inner, precision=HIGH) / jnp.sqrt(jnp.float32(MAXS))
    rotated_ops = turned[:, new_sector]
    return (wavefunction, rotated_ops)
```

```python
import functools

import jax
import jax.numpy as jnp
from jax import lax
from jax.experimental import pallas as pl
from jax.experimental.pallas import tpu as pltpu
from jax.sharding import PartitionSpec as P

F32 = jnp.float32
BF16 = jnp.bfloat16
MESH = pl.DeviceIdType.MESH
TINY = 1e-6
NN = (((1,), (0,)), ((), ()))
NT = (((1,), (1,)), ((), ()))
TN = (((0,), (0,)), ((), ()))


def near_first(count):
    return sorted(range(1, count), key=lambda d: (min(d, count - d), d))


def split(value):
    high = value.astype(BF16)
    low = (value - high.astype(F32)).astype(BF16)
    return high, low


def three_pass(a, b, dims):
    def dot(u, v):
        return lax.dot_general(u, v, dims, preferred_element_type=F32)

    return dot(a[0], b[0]) + (dot(a[0], b[1]) + dot(a[1], b[0]))


def row_of(values):
    rows, columns = values.shape
    folded = values.reshape(rows // 8, 8, columns).sum(axis=0)
    width = min(columns, 128)
    total = folded[:, :width]
    for at in range(width, columns, width):
        total = total + folded[:, at : at + width]
    return jnp.sum(total, axis=0, keepdims=True)


def kernel(
    X,
    Z,
    S,
    states,
    couple,
    labels,
    psi,
    diag,
    left_hbm,
    right_hbm,
    wave,
    rotated,
    left,
    right,
    left_hl,
    right_hl,
    start,
    diags,
    part,
    rs1,
    rs2_out,
    rs2,
    heff,
    corr,
    xnow,
    hnow,
    mixed,
    mixed_in,
    tiles,
    chosen_hl,
    load_sem,
    ex_send,
    ex_recv,
    rs1_send,
    rs1_recv,
    rs2_send,
    rs2_recv,
    ag_send,
    ag_recv,
    side_send,
    side_recv,
    mix_send,
    mix_recv,
    sum_send,
    sum_recv,
):
    N = psi.shape[0]
    Y = S // 2
    w = N // (X * Z)
    ops = lax.axis_index("ops")
    sec = lax.axis_index("sec")
    x, z = ops // Z, ops % Z
    y, core = sec // 2, sec % 2
    partner = y * 2 + (1 - core)
    outer = (sec + 2 * core - 1 + S) % S

    def at_x(d):
        return {"ops": ((x + d) % X) * Z + z, "sec": sec}

    def at_z(d):
        return {"ops": x * Z + (z + d) % Z, "sec": sec}

    sides = ({"ops": ops, "sec": partner}, {"ops": ops, "sec": outer})
    xcore = [({"ops": ((x + d) % X) * Z + z, "sec": y * 2 + c}) for d in range(X) for c in (core, 1 - core)][1:]
    groups = (
        (x * 2 + core, xcore),
        (z, [at_z(d) for d in range(1, Z)]),
        (y, [{"ops": ops, "sec": ((y + d) % Y) * 2 + core} for d in range(1, Y)]),
    )

    barrier = pltpu.get_barrier_semaphore()
    peers = [device for _, members in groups for device in members] + [sides[1]]
    for device in peers:
        pl.semaphore_signal(barrier, inc=1, device_id=device, device_id_type=MESH)

    loads = [
        pltpu.make_async_copy(left_hbm, left, load_sem.at[0]),
        pltpu.make_async_copy(right_hbm, right, load_sem.at[1]),
    ]
    for load in loads:
        load.start()

    size = states[0]
    rows_at = lax.broadcasted_iota(jnp.int32, (N, N), 0)
    cols_at = lax.broadcasted_iota(jnp.int32, (N, N), 1)
    live = ((rows_at < size) & (cols_at < size)).astype(F32)
    start[0] = psi[...].astype(F32) * live
    diags[0] = diag[...].astype(F32)

    pl.semaphore_wait(barrier, len(peers))

    def send(src, dst, send_sem, recv_sem, device):
        copy = pltpu.make_async_remote_copy(
            src_ref=src,
            dst_ref=dst,
            send_sem=send_sem,
            recv_sem=recv_sem,
            device_id=device,
            device_id_type=MESH,
        )
        copy.start()

    def settle(like, sem):
        pltpu.make_async_copy(like, like, sem).wait()

    for j in range(2):
        send(start.at[0], start.at[1 + j], ex_send.at[j], ex_recv.at[j], sides[j])
    for j in range(2):
        send(diags.at[0], diags.at[1 + j], ex_send.at[2 + j], ex_recv.at[2 + j], sides[j])

    for load in loads:
        load.wait()
    for p in range(2):
        left_hl[0, p], left_hl[1, p] = split(left[p])
        right_hl[0, p], right_hl[1, p] = split(right[p])

    picks = []
    for p in range(2):
        source = couple[p]
        row = []
        for target in (sec, partner, outer):
            row.append(jnp.where((source == target) & (source >= 0), 1.0, 0.0).astype(F32))
        picks.append(row)

    def apply(i, v):
        for p in range(2):
            chosen = picks[p][0] * v[0] + picks[p][1] * v[1] + picks[p][2] * v[2]
            chosen_hl[0, p], chosen_hl[1, p] = split(chosen)
        for p in range(2):
            mixed[i, p] = three_pass(
                (left_hl[0, p], left_hl[1, p]), (chosen_hl[0, p], chosen_hl[1, p]), NN
            )
        send(mixed.at[i], mixed_in.at[i], mix_send.at[i], mix_recv.at[i], sides[0])
        total = None
        for p in range(2):
            term = three_pass(split(mixed[i, p]), (right_hl[0, p], right_hl[1, p]), NT)
            total = term if total is None else total + term
        return total

    def slice_of(index):
        return pl.ds(pl.multiple_of(index * w, w), w)

    def scatter_start(i):
        for dz in reversed(near_first(Z)):
            zc = (z + dz) % Z
            for dx in reversed(near_first(X)):
                src = part.at[i, slice_of(((x + dx) % X) * Z + zc)]
                send(src, rs1.at[i, x, zc], rs1_send.at[i], rs1_recv.at[i, zc], at_x(dx))
        for dx in reversed(near_first(X)):
            src = part.at[i, slice_of(((x + dx) % X) * Z + z)]
            send(src, rs1.at[i, x, z], rs1_send.at[i], rs1_recv.at[i, z], at_x(dx))

    def summed_over_x(i, zc):
        settle(rs1.at[i, pl.ds(0, X - 1), 0], rs1_recv.at[i, zc])
        total = part[i, slice_of(x * Z + zc)]
        for dx in range(1, X):
            total = total + rs1[i, (x + dx) % X, zc]
        return total

    def scatter_middle(i):
        for dz in reversed(near_first(Z)):
            zc = (z + dz) % Z
            rs2_out[i, zc] = summed_over_x(i, zc)
            send(rs2_out.at[i, zc], rs2.at[i, z], rs2_send.at[i], rs2_recv.at[i], at_z(dz))
        rs2_out[i, z] = summed_over_x(i, z)

    def scatter_end(i):
        settle(rs2.at[i, pl.ds(0, Z - 1)], rs2_recv.at[i])
        total = rs2_out[i, z]
        for dz in range(1, Z):
            total = total + rs2[i, (z + dz) % Z]
        rows = lax.broadcasted_iota(jnp.int32, (w, N), 0) + ops * w
        cols = lax.broadcasted_iota(jnp.int32, (w, N), 1)
        mask = ((rows < size) & (cols < size)).astype(F32)
        heff[i, 0, slice_of(ops)] = total * mask

    def to_sides(i, index):
        src = heff.at[i, 0, slice_of(index)]
        for j in (1, 0):
            dst = heff.at[i, 1 + j, slice_of(index)]
            send(src, dst, side_send.at[i, j], side_recv.at[i, j], sides[j])

    def gather_start(i):
        src = heff.at[i, 0, slice_of(ops)]
        for dz in reversed(near_first(Z)):
            send(src, src, ag_send.at[i, 0], ag_recv.at[i, ops], at_z(dz))
        for dx in reversed(near_first(X)):
            send(src, src, ag_send.at[i, 1], ag_recv.at[i, ops], at_x(dx))
        to_sides(i, ops)

    def gather_along_x(i):
        for dz in near_first(Z):
            index = x * Z + (z + dz) % Z
            src = heff.at[i, 0, slice_of(index)]
            settle(src, ag_recv.at[i, index])
            for dx in reversed(near_first(X)):
                send(src, src, ag_send.at[i, 1], ag_recv.at[i, index], at_x(dx))
            to_sides(i, index)

    def gather_end(i):
        for dz in [0] + near_first(Z):
            for dx in near_first(X):
                index = ((x + dx) % X) * Z + (z + dz) % Z
                settle(heff.at[i, 0, slice_of(index)], ag_recv.at[i, index])
                to_sides(i, index)
        for j in range(2):
            settle(heff.at[i, 1 + j], side_recv.at[i, j])

    def reduction_sends_done(i):
        for _ in range(X - 1):
            settle(rs1.at[i, 0], rs1_send.at[i])
            settle(rs1.at[i, 0], ag_send.at[i, 1])
        settle(rs2.at[i, pl.ds(0, Z - 1)], rs2_send.at[i])
        settle(rs2.at[i, pl.ds(0, Z - 1)], ag_send.at[i, 0])
        for j in range(2):
            settle(heff.at[i, 0], side_send.at[i, j])

    def sum_start(i, stage, tile):
        mine, members = groups[stage]
        slot = tiles.at[i, stage, mine]
        slot[...] = tile
        for device in members:
            send(slot, slot, sum_send.at[i, stage], sum_recv.at[i, stage], device)

    def sum_end(i, stage):
        others = len(groups[stage][1])
        settle(tiles.at[i, stage, pl.ds(0, others)], sum_recv.at[i, stage])
        total = tiles[i, stage, 0]
        for slot in range(1, others + 1):
            total = total + tiles[i, stage, slot]
        return total

    def sums_done(i):
        for stage in range(3):
            others = len(groups[stage][1])
            settle(tiles.at[i, stage, pl.ds(0, others)], sum_send.at[i, stage])

    def tile_of(values):
        rows = [row_of(value) for value in values]
        blank = jnp.zeros_like(rows[0])
        tile = jnp.concatenate(rows + [blank] * (8 - len(rows)), axis=0)
        if tile.shape[1] < 128:
            tile = jnp.concatenate([tile, jnp.zeros((8, 128 - tile.shape[1]), F32)], axis=1)
        return tile

    def scalars_of(tile, count):
        columns = jnp.sum(tile, axis=1, keepdims=True)
        return [columns[q : q + 1] for q in range(count)]

    share = 1.0 / (X * Z)

    for j in range(2):
        settle(start.at[1 + j], ex_recv.at[j])
    term = apply(0, start)
    part[0] = term
    scatter_start(0)
    own = start[0]
    sum_start(0, 0, tile_of([own * own * share, own * term]))
    scatter_middle(0)
    sum_start(0, 1, sum_end(0, 0))
    scatter_end(0)
    gather_start(0)
    sum_start(0, 2, sum_end(0, 1))
    gather_along_x(0)
    gather_end(0)
    squares, energy = scalars_of(sum_end(0, 2), 2)
    for j in range(2):
        settle(diags.at[1 + j], ex_recv.at[2 + j])

    factor = lax.rsqrt(squares + TINY)
    theta = energy * factor * factor

    for b in range(3):
        top = factor * heff[0, b] - theta * (factor * start[b])
        corr[0, b] = top / (jnp.abs(diags[b] - theta) + 1.0)

    def turn(tile, theta):
        xt, ct, k, cc, chx, xx, xhx = scalars_of(tile, 7)
        square = jnp.maximum(cc - 2.0 * k * k + k * k * xx, 0.0)
        n = lax.rsqrt(square + TINY)
        middle = 0.5 * n * ((xt - k * xhx) + (chx - k * xhx))
        last = n * n * (ct - k * xt - k * chx + k * k * xhx)
        u, v = last - theta, -2.0 * middle
        most = jnp.maximum(jnp.abs(u), jnp.abs(v))
        safe = jnp.where(most > 0.0, most, 1.0)
        us, vs = u / safe, v / safe
        r = jnp.sqrt(us * us + vs * vs)
        rs = jnp.where(most > 0.0, r, 1.0)
        big = jnp.sqrt(0.5 * (rs + jnp.abs(us)) / rs)
        small = 0.5 * jnp.abs(vs) / (rs * big)
        sign = jnp.where(middle >= 0.0, -1.0, 1.0)
        cosine = jnp.where(u >= 0.0, big, small)
        sine = sign * jnp.where(u >= 0.0, small, big)
        cosine = jnp.where(most > 0.0, cosine, 1.0)
        sine = jnp.where(most > 0.0, sine, 0.0)
        lowest = 0.5 * (theta + last) - 0.5 * jnp.where(most > 0.0, safe * r, 0.0)
        return cosine - sine * n * k, sine * n, lowest

    term = apply(1, corr.at[0])
    part[1] = term
    scatter_start(1)
    own, hown, c = factor * start[0], factor * heff[0, 0], corr[0, 0]
    sum_start(
        1,
        0,
        tile_of(
            [
                own * term,
                c * term,
                own * c * share,
                c * c * share,
                c * hown * share,
                own * own * share,
                own * hown * share,
            ]
        ),
    )
    scatter_middle(1)
    sum_start(1, 1, sum_end(1, 0))
    scatter_end(1)
    gather_start(1)
    sum_start(1, 2, sum_end(1, 1))
    gather_along_x(1)
    gather_end(1)
    alpha, beta, theta = turn(sum_end(1, 2), theta)
    alpha = alpha * factor
    hown = None
    for b in range(3):
        xb = alpha * start[b] + beta * corr[0, b]
        hb = alpha * heff[0, b] + beta * heff[1, b]
        xnow[b] = xb
        corr[1, b] = (hb - theta * xb) / (jnp.abs(diags[b] - theta) + 1.0)
        if hown is None:
            hown = hb
    hnow[...] = hown

    term = apply(2, corr.at[1])
    own, hown, c = xnow[0], hnow[...], corr[1, 0]
    sum_start(
        2,
        0,
        tile_of(
            [
                own * term,
                c * term,
                own * c * share,
                c * c * share,
                c * hown * share,
                own * own * share,
                own * hown * share,
            ]
        ),
    )
    keep = jnp.where(labels[0] == sec, 1.0, 0.0).astype(F32)
    swap = 1.0 - keep
    for i in range(3):
        settle(mixed_in.at[i], mix_recv.at[i])
        settle(mixed_in.at[i], mix_send.at[i])
    for p in range(2):
        first = alpha * mixed[0, p] + beta * mixed[1, p]
        other = alpha * mixed_in[0, p] + beta * mixed_in[1, p]
        left[p] = keep * first + swap * other
        right[p] = keep * mixed[2, p] + swap * mixed_in[2, p]
    sum_start(2, 1, sum_end(2, 0))
    sum_start(2, 2, sum_end(2, 1))
    for i in range(2):
        reduction_sends_done(i)
    for j in range(2):
        settle(start.at[0], ex_send.at[j])
        settle(diags.at[0], ex_send.at[2 + j])
    for i in range(2):
        sums_done(i)
    alpha, beta, theta = turn(sum_end(2, 2), theta)
    scale = jnp.sqrt(jnp.float32(S * N * N))
    alpha, beta = alpha * scale, beta * scale
    wave_own = alpha * xnow[0] + beta * corr[1, 0]
    wave[...] = wave_own
    basis = keep * wave_own + swap * (alpha * xnow[1] + beta * corr[1, 1])
    basis = split(basis * (1.0 / jnp.sqrt(jnp.float32(N))))
    for p in range(2):
        inner = split(alpha * left[p] + beta * right[p])
        rotated[p] = three_pass(basis, inner, TN)
    sums_done(2)


def local(X, sector_states, psi_guess, precond_diag, left_ops, right_ops, couple, new_sector):
    N = psi_guess.shape[1]
    S = lax.axis_size("sec")
    Z = lax.axis_size("ops") // X
    pairs = left_ops.shape[0]
    w = N // (X * Z)
    G = max(2 * X, Z, S // 2)
    dma = pltpu.SemaphoreType.DMA
    smem = pl.BlockSpec(memory_space=pltpu.SMEM)
    vmem = pl.BlockSpec(memory_space=pltpu.VMEM)
    hbm = pl.BlockSpec(memory_space=pl.ANY)
    wave, rotated = pl.pallas_call(
        functools.partial(kernel, X, Z, S),
        out_shape=(
            jax.ShapeDtypeStruct((N, N), F32),
            jax.ShapeDtypeStruct((pairs, N, N), F32),
        ),
        in_specs=[smem, smem, smem, vmem, vmem, hbm, hbm],
        out_specs=(vmem, vmem),
        scratch_shapes=[
            pltpu.VMEM((2, N, N), F32),
            pltpu.VMEM((2, N, N), F32),
            pltpu.VMEM((2, 2, N, N), BF16),
            pltpu.VMEM((2, 2, N, N), BF16),
            pltpu.VMEM((3, N, N), F32),
            pltpu.VMEM((3, N, N), F32),
            pltpu.VMEM((2, N, N), F32),
            pltpu.VMEM((2, X, Z, w, N), F32),
            pltpu.VMEM((2, Z, w, N), F32),
            pltpu.VMEM((2, Z, w, N), F32),
            pltpu.VMEM((2, 3, N, N), F32),
            pltpu.VMEM((2, 3, N, N), F32),
            pltpu.VMEM((3, N, N), F32),
            pltpu.VMEM((N, N), F32),
            pltpu.VMEM((3, 2, N, N), F32),
            pltpu.VMEM((3, 2, N, N), F32),
            pltpu.VMEM((3, 3, G, 8, 128), F32),
            pltpu.VMEM((2, 2, N, N), BF16),
            dma((2,)),
            dma((4,)),
            dma((4,)),
            dma((2,)),
            dma((2, Z)),
            dma((2,)),
            dma((2,)),
            dma((2, 2)),
            dma((2, X * Z)),
            dma((2, 2)),
            dma((2, 2)),
            dma((3,)),
            dma((3,)),
            dma((3, 3)),
            dma((3, 3)),
        ],
        compiler_params=pltpu.CompilerParams(collective_id=0, has_side_effects=True),
    )(
        sector_states,
        couple[:, 0],
        new_sector,
        psi_guess[0],
        precond_diag[0],
        left_ops[:, 0],
        right_ops[:, 0],
    )
    return wave[None], rotated[:, None]


def solution(mesh):
    count = mesh.shape["ops"]
    X = 4 if count == 32 else 2
    in_specs = (
        P("sec"),
        P("sec", None, None),
        P("sec", None, None),
        P("ops", "sec", None, None),
        P("ops", "sec", None, None),
        P("ops", "sec"),
        P("sec"),
    )
    out_specs = (P("sec", None, None), P("ops", "sec", None, None))
    return jax.shard_map(
        functools.partial(local, X), mesh=mesh, in_specs=in_specs, out_specs=out_specs, check_vma=False
    )
```

```python
import functools

import jax
import jax.numpy as jnp
from jax import lax
from jax.experimental import pallas as pl
from jax.experimental.pallas import tpu as pltpu
from jax.sharding import PartitionSpec as P

F32 = jnp.float32
BF16 = jnp.bfloat16
MESH = pl.DeviceIdType.MESH
TINY = 1e-6
FAR = 9
BULK = True
HAND_ON = True
NN = (((1,), (0,)), ((), ()))
TN = (((0,), (0,)), ((), ()))


def near_first(count):
    return sorted(range(1, count), key=lambda d: (min(d, count - d), d))


def split(value):
    high = value.astype(BF16)
    low = (value - high.astype(F32)).astype(BF16)
    return high, low


def dot(a, b, dims=NN):
    return lax.dot_general(a, b, dims, preferred_element_type=F32)


def row_of(values):
    rows, columns = values.shape
    folded = values.reshape(rows // 8, 8, columns).sum(axis=0)
    width = min(columns, 128)
    total = folded[:, :width]
    for at in range(width, columns, width):
        total = total + folded[:, at : at + width]
    return jnp.sum(total, axis=0, keepdims=True)


def tile_of(values):
    rows = [row_of(value) for value in values]
    blank = jnp.zeros_like(rows[0])
    tile = jnp.concatenate(rows + [blank] * (8 - len(rows)), axis=0)
    if tile.shape[1] < 128:
        tile = jnp.concatenate([tile, jnp.zeros((8, 128 - tile.shape[1]), F32)], axis=1)
    return tile


def scalars_of(tile, count):
    columns = jnp.sum(tile, axis=1, keepdims=True)
    return [columns[q : q + 1] for q in range(count)]


def turn(tile, theta):
    xt, ct, k, cc, chx, xx, xhx = scalars_of(tile, 7)
    square = jnp.maximum(cc - 2.0 * k * k + k * k * xx, 0.0)
    n = lax.rsqrt(square + TINY)
    middle = 0.5 * n * ((xt - k * xhx) + (chx - k * xhx))
    last = n * n * (ct - k * xt - k * chx + k * k * xhx)
    u, v = last - theta, -2.0 * middle
    most = jnp.maximum(jnp.abs(u), jnp.abs(v))
    safe = jnp.where(most > 0.0, most, 1.0)
    us, vs = u / safe, v / safe
    r = jnp.sqrt(us * us + vs * vs)
    rs = jnp.where(most > 0.0, r, 1.0)
    big = jnp.sqrt(0.5 * (rs + jnp.abs(us)) / rs)
    small = 0.5 * jnp.abs(vs) / (rs * big)
    sign = jnp.where(middle >= 0.0, -1.0, 1.0)
    cosine = jnp.where(u >= 0.0, big, small)
    sine = sign * jnp.where(u >= 0.0, small, big)
    cosine = jnp.where(most > 0.0, cosine, 1.0)
    sine = jnp.where(most > 0.0, sine, 0.0)
    lowest = 0.5 * (theta + last) - 0.5 * jnp.where(most > 0.0, safe * r, 0.0)
    return cosine - sine * n * k, sine * n, lowest


SCRATCH = (
    "left",
    "right",
    "left_cat",
    "right_cat",
    "chosen_cat",
    "mixed_cat",
    "start",
    "diags",
    "gain",
    "shift",
    "partial",
    "part",
    "rs_x",
    "rs_far",
    "rs_out",
    "rs_z",
    "heff",
    "corr",
    "xnow",
    "hnow",
    "mixed",
    "mixed_in",
    "tiles",
    "load_sem",
    "ex_send",
    "ex_recv",
    "rsx_send",
    "rsx_recv",
    "rsf_send",
    "rsf_recv",
    "rsz_send",
    "rsz_recv",
    "agz_send",
    "agx_send",
    "agf_send",
    "ag_recv",
    "side_send",
    "side_recv",
    "mix_send",
    "mix_recv",
    "sum_send",
    "sum_recv",
    "wide_tiles",
    "wide_send",
    "wide_recv",
    "local_tile",
    "turn_cat",
    "quad",
)


def kernel(X, Z, S, states, couple, labels, psi, diag, left_hbm, right_hbm, wave, rotated, *scratch):
    refs = dict(zip(SCRATCH, scratch, strict=True))
    left, right, left_cat, right_cat = (refs[k] for k in SCRATCH[:4])
    chosen_cat, mixed_cat, start, diags, gain, shift, partial, part = (refs[k] for k in SCRATCH[4:12])
    rs_x, rs_far, rs_out, rs_z, heff, corr, xnow, hnow, mixed, mixed_in, tiles = (refs[k] for k in SCRATCH[12:23])
    load_sem, ex_send, ex_recv, rsx_send, rsx_recv, rsf_send, rsf_recv = (refs[k] for k in SCRATCH[23:30])
    rsz_send, rsz_recv, agz_send, agx_send, agf_send, ag_recv, side_send = (refs[k] for k in SCRATCH[30:37])
    side_recv, mix_send, mix_recv, sum_send, sum_recv, wide_tiles, wide_send, wide_recv = (
        refs[k] for k in SCRATCH[37:45]
    )
    local_tile, turn_cat, quad = (refs[k] for k in SCRATCH[45:])
    N = psi.shape[0]
    Y = S // 2
    w = N // (X * Z)
    block = N // X
    ops = lax.axis_index("ops")
    sec = lax.axis_index("sec")
    x, z = ops // Z, ops % Z
    y, core = sec // 2, sec % 2
    partner = y * 2 + (1 - core)
    outer = (sec + 2 * core - 1 + S) % S
    far = [d for d in reversed(near_first(Z)) if min(d, Z - d) >= FAR]
    near = [d for d in near_first(Z) if d not in far]
    around = near_first(X)

    def at(xd, zd):
        return {"ops": xd * Z + zd, "sec": sec}

    def off(dx, dz):
        return at((x + dx) % X, (z + dz) % Z)

    sides = ({"ops": ops, "sec": partner}, {"ops": ops, "sec": outer})
    xcore = [{"ops": ((x + d) % X) * Z + z, "sec": y * 2 + c} for d in range(X) for c in (core, 1 - core)][1:]
    groups = (
        (x * 2 + core, xcore),
        (z, [off(0, d) for d in range(1, Z)]),
        (y, [{"ops": ops, "sec": ((y + d) % Y) * 2 + core} for d in range(1, Y)]),
    )

    plane = [(dx, dz) for dz in reversed([0] + near_first(Z)) for dx in reversed([0] + around) if dx or dz]
    wide_groups = (
        (ops, [off(dx, dz) for dx, dz in plane]),
        (
            sec,
            [
                {"ops": ops, "sec": ((y + d) % Y) * 2 + c}
                for d in reversed([0] + near_first(Y))
                for c in ((1 - core, core) if d else (1 - core,))
            ],
        ),
    )

    barrier = pltpu.get_barrier_semaphore()
    peers = [device for _, members in groups for device in members] + [sides[1]]
    peers += [off(dx, dz) for dx in around for dz in far]
    for device in peers:
        pl.semaphore_signal(barrier, inc=1, device_id=device, device_id_type=MESH)

    loads = [
        pltpu.make_async_copy(left_hbm, left, load_sem.at[0]),
        pltpu.make_async_copy(right_hbm, right, load_sem.at[1]),
    ]
    for load in loads:
        load.start()

    size = states[0]
    rows_at = lax.broadcasted_iota(jnp.int32, (N, N), 0)
    cols_at = lax.broadcasted_iota(jnp.int32, (N, N), 1)
    live = ((rows_at < size) & (cols_at < size)).astype(F32)
    start[0] = psi[...].astype(F32) * live
    diags[0] = diag[...].astype(F32)

    pl.semaphore_wait(barrier, len(peers))

    def send(src, dst, send_sem, recv_sem, device):
        copy = pltpu.make_async_remote_copy(
            src_ref=src,
            dst_ref=dst,
            send_sem=send_sem,
            recv_sem=recv_sem,
            device_id=device,
            device_id_type=MESH,
        )
        copy.start()

    def settle(like, sem):
        pltpu.make_async_copy(like, like, sem).wait()

    for g in range(X):
        rows = pl.ds(g * block, block)
        send(start.at[0, rows], start.at[2, rows], ex_send.at[0], ex_recv.at[g], sides[1])
    send(start.at[0], start.at[1], ex_send.at[1], ex_recv.at[X], sides[0])

    for load in loads:
        load.wait()
    for p in range(2):
        high, low = split(left[p])
        for q, piece in enumerate((high, high, low)):
            left_cat[p, :, q * N : (q + 1) * N] = piece
        high, low = split(right[p].T)
        for q, piece in enumerate((high, low, high)):
            right_cat[(3 * p + q) * N : (3 * p + q + 1) * N] = piece

    picks = []
    for p in range(2):
        source = couple[p]
        row = []
        for target in (sec, partner, outer):
            row.append(jnp.where((source == target) & (source >= 0), 1.0, 0.0).astype(F32))
        picks.append(row)

    def choose_inner(own, other):
        for p in range(2):
            partial[p] = picks[p][0] * own + picks[p][1] * other

    def choose_outer(rows_from, value):
        for p in range(2):
            high, low = split(partial[p, pl.ds(rows_from, block)] + picks[p][2] * value)
            for q, piece in enumerate((high, low, high)):
                chosen_cat[p, pl.ds(q * N + rows_from, block)] = piece

    half = X // 2
    upper = x // half

    def apply_half(i, which):
        rows = pl.ds(pl.multiple_of(which * (N // 2), N // 2), N // 2)
        for p in range(2):
            value = dot(left_cat[p, rows], chosen_cat[p])
            mixed[i, p, rows] = value
            high, low = split(value)
            for q, piece in enumerate((high, high, low)):
                mixed_cat[:, (3 * p + q) * N : (3 * p + q + 1) * N] = piece
        part[i, rows] = dot(mixed_cat[...], right_cat[...])

    def slice_of(index):
        return pl.ds(pl.multiple_of(index * w, w), w)

    def scatter_to(i, xd):
        for f, dz in enumerate(far):
            zd = (z + dz) % Z
            send(part.at[i, slice_of(xd * Z + zd)], rs_far.at[i, x, f], rsf_send.at[i], rsf_recv.at[i], at(xd, zd))

    def scatter_along(i, xd):
        for k, dz in reversed(list(enumerate([0] + near))):
            src = part.at[i, slice_of(xd * Z + (z + dz) % Z)]
            send(src, rs_x.at[i, x, k], rsx_send.at[i], rsx_recv.at[i, k], at(xd, z))

    def apply(i, scatter):
        apply_half(i, 1 - upper)
        away = [(1 - upper) * half + j for j in range(half)]
        beside = [x + 1 - 2 * (x % 2)] if half == 2 else []
        if scatter:
            for xd in away:
                scatter_to(i, xd)
                scatter_along(i, xd)
        apply_half(i, upper)
        if scatter:
            for xd in beside + [x]:
                scatter_to(i, xd)
            for xd in beside:
                scatter_along(i, xd)
        send(mixed.at[i], mixed_in.at[i], mix_send.at[i], mix_recv.at[i], sides[0])

    def summed_over_x(i, k, dz):
        settle(rs_x.at[i, pl.ds(0, X - 1), 0], rsx_recv.at[i, k])
        total = part[i, slice_of(x * Z + (z + dz) % Z)]
        for dx in range(1, X):
            total = total + rs_x[i, (x + dx) % X, k]
        return total

    def scatter_middle(i):
        for k, dz in reversed(list(enumerate([0] + near))):
            rs_out[i, k] = summed_over_x(i, k, dz)
            if k > 0:
                send(rs_out.at[i, k], rs_z.at[i, k], rsz_send.at[i], rsz_recv.at[i], off(0, dz))

    def scatter_end(i):
        total = rs_out[i, 0]
        if near:
            settle(rs_z.at[i, pl.ds(0, len(near))], rsz_recv.at[i])
            for k in range(1, len(near) + 1):
                total = total + rs_z[i, k]
        if far:
            settle(rs_far.at[i], rsf_recv.at[i])
            for xs in range(X):
                for f in range(len(far)):
                    total = total + rs_far[i, xs, f]
        rows = lax.broadcasted_iota(jnp.int32, (w, N), 0) + ops * w
        cols = lax.broadcasted_iota(jnp.int32, (w, N), 1)
        mask = ((rows < size) & (cols < size)).astype(F32)
        heff[i, 0, slice_of(ops)] = total * mask

    def to_sides(i, dx, index):
        src = heff.at[i, 0, slice_of(index)]
        send(src, heff.at[i, 2, slice_of(index)], side_send.at[i, 1], side_recv.at[i, 1 + dx], sides[1])
        if not BULK:
            send(src, heff.at[i, 1, slice_of(index)], side_send.at[i, 0], side_recv.at[i, 0], sides[0])

    def gather_start(i):
        src = heff.at[i, 0, slice_of(ops)]
        for dz in far:
            for dx in list(reversed(around)) + [0]:
                send(src, src, agf_send.at[i], ag_recv.at[i, ops], off(dx, dz))
        for dz in reversed(near):
            send(src, src, agz_send.at[i], ag_recv.at[i, ops], off(0, dz))
        for dx in reversed(around):
            send(src, src, agx_send.at[i], ag_recv.at[i, ops], off(dx, 0))
        to_sides(i, 0, ops)

    def gather_along_x(i):
        for dz in near:
            index = x * Z + (z + dz) % Z
            src = heff.at[i, 0, slice_of(index)]
            settle(src, ag_recv.at[i, index])
            for dx in reversed(around):
                send(src, src, agx_send.at[i], ag_recv.at[i, index], off(dx, 0))
            to_sides(i, 0, index)

    def gather_end(i):
        rest = [(dx, 0) for dx in around] + [(0, dz) for dz in reversed(far)]
        rest += [(dx, dz) for dz in near for dx in around]
        rest += [(dx, dz) for dz in reversed(far) for dx in around]
        for dx, dz in rest:
            index = ((x + dx) % X) * Z + (z + dz) % Z
            settle(heff.at[i, 0, slice_of(index)], ag_recv.at[i, index])
            to_sides(i, dx, index)
        if BULK:
            send(heff.at[i, 0], heff.at[i, 1], side_send.at[i, 0], side_recv.at[i, 0], sides[0])

    def reduction_sends_done(i):
        for _ in range(X - 1):
            settle(rs_x.at[i, 0, pl.ds(0, 1 + len(near))], rsx_send.at[i])
            settle(rs_x.at[i, 0, pl.ds(0, 1 + len(near))], agx_send.at[i])
        if far:
            settle(rs_far.at[i], rsf_send.at[i])
            settle(rs_far.at[i], agf_send.at[i])
        if near:
            settle(rs_z.at[i, pl.ds(0, len(near))], rsz_send.at[i])
            settle(rs_z.at[i, pl.ds(0, len(near))], agz_send.at[i])
        for j in range(2):
            settle(heff.at[i, 0], side_send.at[i, j])

    def sum_start(i, stage, tile):
        mine, members = groups[stage]
        slot = tiles.at[i, stage, mine]
        slot[...] = tile
        for device in members:
            send(slot, slot, sum_send.at[i, stage], sum_recv.at[i, stage], device)

    def sum_end(i, stage):
        others = len(groups[stage][1])
        settle(tiles.at[i, stage, pl.ds(0, others)], sum_recv.at[i, stage])
        total = tiles[i, stage, 0]
        for slot in range(1, others + 1):
            total = total + tiles[i, stage, slot]
        return total

    def sums_done(i):
        for stage in range(3):
            others = len(groups[stage][1])
            settle(tiles.at[i, stage, pl.ds(0, others)], sum_send.at[i, stage])

    def wide_start(stage, row):
        mine, members = wide_groups[stage]
        slot = wide_tiles.at[stage, mine]
        slot[...] = row
        for device in members:
            send(slot, slot, wide_send.at[stage], wide_recv.at[stage], device)

    def wide_end(stage):
        others = len(wide_groups[stage][1])
        settle(wide_tiles.at[stage, pl.ds(0, others)], wide_recv.at[stage])
        totals = [wide_tiles[stage, slot] for slot in range(others + 1)]
        while len(totals) > 1:
            totals = [sum(totals[j : j + 2]) for j in range(0, len(totals), 2)]
        return totals[0]

    def wide_done(stage):
        others = len(wide_groups[stage][1])
        settle(wide_tiles.at[stage, pl.ds(0, others)], wide_send.at[stage])

    lane = lax.broadcasted_iota(jnp.int32, (8, 128), 1)
    sublane = lax.broadcasted_iota(jnp.int32, (8, 128), 0)

    def packed(tile):
        columns = jnp.sum(tile, axis=1, keepdims=True)
        return jnp.sum(jnp.where(lane == sublane, columns, 0.0), axis=0, keepdims=True)

    def unpacked(row):
        return jnp.where(lane == sublane, row, 0.0)

    share = 1.0 / (X * Z)

    def reduce(i, tile):
        sum_start(i, 0, tile)
        scatter_middle(i)
        sum_start(i, 1, sum_end(i, 0))
        scatter_end(i)
        gather_start(i)
        sum_start(i, 2, sum_end(i, 1))
        gather_along_x(i)
        gather_end(i)

    def correct(i, own, hown):
        c = gain[0] * heff[i, 0] - shift[0]
        corr[i, 0] = c
        settle(heff.at[i, 1], side_recv.at[i, 0])
        corr[i, 1] = gain[1] * heff[i, 1] - shift[1]
        choose_inner(corr[i, 0], corr[i, 1])
        rest = [value * share for value in (own * c, c * c, c * hown, own * own, own * hown)]
        local_tile[...] = tile_of([jnp.zeros_like(own)] * 2 + rest)
        for dx in [0] + around:
            rows_from = pl.multiple_of(((x + dx) % X) * block, block)
            rows = pl.ds(rows_from, block)
            settle(heff.at[i, 2, rows], side_recv.at[i, 1 + dx])
            value = gain[2, rows] * heff[i, 2, rows] - shift[2, rows]
            corr[i, 2, rows] = value
            choose_outer(rows_from, value)

    settle(start.at[1], ex_recv.at[X])
    choose_inner(start[0], start[1])
    for g in range(X):
        rows = pl.ds(g * block, block)
        settle(start.at[2, rows], ex_recv.at[g])
        choose_outer(g * block, start[2, rows])
    apply(0, True)
    for j in range(2):
        send(diags.at[0], diags.at[1 + j], ex_send.at[2 + j], ex_recv.at[X + 1 + j], sides[j])
    own, term = start[0], part[0]
    reduce(0, tile_of([own * own * share, own * term]))
    squares, energy = scalars_of(sum_end(0, 2), 2)
    factor = lax.rsqrt(squares + TINY)
    theta = energy * factor * factor
    for j in range(2):
        settle(diags.at[1 + j], ex_recv.at[X + 1 + j])
    for b in range(3):
        inverse = 1.0 / (jnp.abs(diags[b] - theta) + 1.0)
        gain[b] = factor * inverse
        shift[b] = (theta * factor) * start[b] * inverse
    correct(0, factor * start[0], factor * heff[0, 0])

    def products(term, own, c):
        return local_tile[...] + tile_of([own * term, c * term])

    apply(1, True)
    reduce(1, products(part[1], factor * start[0], corr[0, 0]))
    alpha, beta, theta = turn(sum_end(1, 2), theta)
    alpha = alpha * factor
    for b in range(3):
        xb = alpha * start[b] + beta * corr[0, b]
        inverse = 1.0 / (jnp.abs(diags[b] - theta) + 1.0)
        xnow[b] = xb
        gain[b] = beta * inverse
        shift[b] = (theta * xb - alpha * heff[0, b]) * inverse
    hnow[...] = alpha * heff[0, 0] + beta * heff[1, 0]
    correct(1, xnow[0], hnow[...])

    apply(2, False)
    wide_start(0, packed(products(part[2], xnow[0], corr[1, 0])))
    keep = jnp.where(labels[0] == sec, 1.0, 0.0).astype(F32)
    swap = 1.0 - keep
    for i in range(3):
        settle(mixed_in.at[i], mix_recv.at[i])
        settle(mixed_in.at[i], mix_send.at[i])
    root = 1.0 / jnp.sqrt(jnp.float32(N))
    sources = (xnow, corr.at[1])
    for q, source in enumerate(sources):
        value = (keep * source[0] + swap * source[1]) * root
        turn_cat[q, 0], turn_cat[q, 1] = split(value.T)

    def turned_by(q, value):
        high, low = value
        return dot(turn_cat[q, 0], high) + (dot(turn_cat[q, 0], low) + dot(turn_cat[q, 1], high))

    def quadratic(p):
        first = alpha * mixed[0, p] + beta * mixed[1, p]
        other = alpha * mixed_in[0, p] + beta * mixed_in[1, p]
        first = split(keep * first + swap * other)
        second = split(keep * mixed[2, p] + swap * mixed_in[2, p])
        quad[p, 0] = turned_by(0, first)
        quad[p, 1] = turned_by(0, second) + turned_by(1, first)
        quad[p, 2] = turned_by(1, second)

    quadratic(0)
    wide_start(1, wide_end(0))
    quadratic(1)
    for i in range(2):
        reduction_sends_done(i)
        sums_done(i)
    for j in range(2):
        settle(start.at[0], ex_send.at[j])
        settle(diags.at[0], ex_send.at[2 + j])
    wide_done(0)
    alpha, beta, theta = turn(unpacked(wide_end(1)), theta)
    scale = jnp.sqrt(jnp.float32(S * N * N))
    alpha, beta = alpha * scale, beta * scale
    wave[...] = alpha * xnow[0] + beta * corr[1, 0]
    aa, ab, bb = alpha * alpha, alpha * beta, beta * beta
    for p in range(2):
        rotated[p] = (aa * quad[p, 0] + ab * quad[p, 1]) + bb * quad[p, 2]
    wide_done(1)


def handed_on(wave, rotated, wave_out, rotated_out):
    wave_out[...] = wave[...]
    rotated_out[...] = rotated[...]


def local(X, sector_states, psi_guess, precond_diag, left_ops, right_ops, couple, new_sector):
    N = psi_guess.shape[1]
    S = lax.axis_size("sec")
    Z = lax.axis_size("ops") // X
    pairs = left_ops.shape[0]
    w = N // (X * Z)
    G = max(2 * X, Z, S // 2)
    F = max(1, sum(min(d, Z - d) >= FAR for d in range(1, Z)))
    dma = pltpu.SemaphoreType.DMA
    smem = pl.BlockSpec(memory_space=pltpu.SMEM)
    vmem = pl.BlockSpec(memory_space=pltpu.VMEM)
    hbm = pl.BlockSpec(memory_space=pl.ANY)
    shapes = {
        "left": (2, N, N),
        "right": (2, N, N),
        "left_cat": (2, N, 3 * N),
        "right_cat": (6 * N, N),
        "chosen_cat": (2, 3 * N, N),
        "mixed_cat": (N // 2, 6 * N),
        "start": (3, N, N),
        "diags": (3, N, N),
        "gain": (3, N, N),
        "shift": (3, N, N),
        "partial": (2, N, N),
        "part": (3, N, N),
        "rs_x": (2, X, Z, w, N),
        "rs_far": (2, X, F, w, N),
        "rs_out": (2, Z, w, N),
        "rs_z": (2, Z, w, N),
        "heff": (2, 3, N, N),
        "corr": (2, 3, N, N),
        "xnow": (3, N, N),
        "hnow": (N, N),
        "mixed": (3, 2, N, N),
        "mixed_in": (3, 2, N, N),
        "tiles": (2, 3, G, 8, 128),
        "local_tile": (8, 128),
        "turn_cat": (2, 2, N, N),
        "quad": (2, 3, N, N),
        "wide_tiles": (2, max(X * Z, S), 1, 128),
    }
    sems = {
        "load_sem": (2,),
        "ex_send": (4,),
        "ex_recv": (X + 3,),
        "rsx_recv": (2, Z),
        "ag_recv": (2, X * Z),
        "side_send": (2, 2),
        "side_recv": (2, 1 + X),
        "mix_send": (3,),
        "mix_recv": (3,),
        "sum_send": (3, 3),
        "sum_recv": (3, 3),
    }
    scratch = []
    for name in SCRATCH:
        if name in shapes:
            scratch.append(pltpu.VMEM(shapes[name], BF16 if name.endswith("_cat") else F32))
        else:
            scratch.append(dma(sems.get(name, (2,))))
    outs = (
        jax.ShapeDtypeStruct((N, N), F32),
        jax.ShapeDtypeStruct((pairs, N, N), F32),
    )
    wave, rotated = pl.pallas_call(
        functools.partial(kernel, X, Z, S),
        out_shape=(pltpu.VMEM((N, N), F32), pltpu.VMEM((pairs, N, N), F32)),
        in_specs=[smem, smem, smem, vmem, vmem, hbm, hbm],
        out_specs=(vmem, vmem),
        scratch_shapes=scratch,
        compiler_params=pltpu.CompilerParams(collective_id=0, has_side_effects=True),
    )(
        sector_states,
        couple[:, 0],
        new_sector,
        psi_guess[0],
        precond_diag[0],
        left_ops[:, 0],
        right_ops[:, 0],
    )
    if HAND_ON:
        wave, rotated = pl.pallas_call(
            handed_on, out_shape=outs, in_specs=[vmem, vmem], out_specs=(vmem, vmem)
        )(*(pltpu.with_memory_space_constraint(value, pltpu.VMEM) for value in (wave, rotated)))
    return wave[None], rotated[:, None]


def solution(mesh):
    count = mesh.shape["ops"]
    X = 4 if count == 32 else 2
    in_specs = (
        P("sec"),
        P("sec", None, None),
        P("sec", None, None),
        P("ops", "sec", None, None),
        P("ops", "sec", None, None),
        P("ops", "sec"),
        P("sec"),
    )
    out_specs = (P("sec", None, None), P("ops", "sec", None, None))
    return jax.shard_map(
        functools.partial(local, X), mesh=mesh, in_specs=in_specs, out_specs=out_specs, check_vma=False
    )
```

```python
import functools

import jax
import jax.numpy as jnp
from jax import lax
from jax.experimental import pallas as pl
from jax.experimental.pallas import tpu as pltpu
from jax.sharding import PartitionSpec as P

F32 = jnp.float32
BF16 = jnp.bfloat16
MESH = pl.DeviceIdType.MESH
TINY = 1e-6
FAR = 9
BULK = True
HAND_ON = True
NN = (((1,), (0,)), ((), ()))
TN = (((0,), (0,)), ((), ()))


def near_first(count):
    return sorted(range(1, count), key=lambda d: (min(d, count - d), d))


def split(value):
    high = value.astype(BF16)
    low = (value - high.astype(F32)).astype(BF16)
    return high, low


def dot(a, b, dims=NN):
    return lax.dot_general(a, b, dims, preferred_element_type=F32)


def row_of(values):
    rows, columns = values.shape
    folded = values.reshape(rows // 8, 8, columns).sum(axis=0)
    width = min(columns, 128)
    total = folded[:, :width]
    for at in range(width, columns, width):
        total = total + folded[:, at : at + width]
    return jnp.sum(total, axis=0, keepdims=True)


def tile_of(values):
    rows = [row_of(value) for value in values]
    blank = jnp.zeros_like(rows[0])
    tile = jnp.concatenate(rows + [blank] * (8 - len(rows)), axis=0)
    if tile.shape[1] < 128:
        tile = jnp.concatenate([tile, jnp.zeros((8, 128 - tile.shape[1]), F32)], axis=1)
    return tile


def scalars_of(tile, count):
    columns = jnp.sum(tile, axis=1, keepdims=True)
    return [columns[q : q + 1] for q in range(count)]


def turn(tile, theta):
    xt, ct, k, cc, chx, xx, xhx = scalars_of(tile, 7)
    square = jnp.maximum(cc - 2.0 * k * k + k * k * xx, 0.0)
    n = lax.rsqrt(square + TINY)
    middle = 0.5 * n * ((xt - k * xhx) + (chx - k * xhx))
    last = n * n * (ct - k * xt - k * chx + k * k * xhx)
    u, v = last - theta, -2.0 * middle
    most = jnp.maximum(jnp.abs(u), jnp.abs(v))
    safe = jnp.where(most > 0.0, most, 1.0)
    us, vs = u / safe, v / safe
    r = jnp.sqrt(us * us + vs * vs)
    rs = jnp.where(most > 0.0, r, 1.0)
    big = jnp.sqrt(0.5 * (rs + jnp.abs(us)) / rs)
    small = 0.5 * jnp.abs(vs) / (rs * big)
    sign = jnp.where(middle >= 0.0, -1.0, 1.0)
    cosine = jnp.where(u >= 0.0, big, small)
    sine = sign * jnp.where(u >= 0.0, small, big)
    cosine = jnp.where(most > 0.0, cosine, 1.0)
    sine = jnp.where(most > 0.0, sine, 0.0)
    lowest = 0.5 * (theta + last) - 0.5 * jnp.where(most > 0.0, safe * r, 0.0)
    return cosine - sine * n * k, sine * n, lowest


SCRATCH = (
    "left",
    "right",
    "left_cat",
    "right_cat",
    "chosen_cat",
    "mixed_cat",
    "start",
    "diags",
    "gain",
    "shift",
    "partial",
    "part",
    "rs_x",
    "rs_far",
    "rs_out",
    "rs_z",
    "heff",
    "corr",
    "xnow",
    "hnow",
    "mixed",
    "mixed_in",
    "tiles",
    "load_sem",
    "ex_send",
    "ex_recv",
    "rsx_send",
    "rsx_recv",
    "rsf_send",
    "rsf_recv",
    "rsz_send",
    "rsz_recv",
    "agz_send",
    "agx_send",
    "agf_send",
    "ag_recv",
    "side_send",
    "side_recv",
    "mix_send",
    "mix_recv",
    "sum_send",
    "sum_recv",
    "wide_tiles",
    "wide_send",
    "wide_recv",
    "local_tile",
    "turn_cat",
    "quad",
    "psi",
    "diag",
)


def kernel(X, Z, S, states, couple, labels, psi_hbm, diag_hbm, left_hbm, right_hbm, wave, rotated, *scratch):
    refs = dict(zip(SCRATCH, scratch, strict=True))
    left, right, left_cat, right_cat = (refs[k] for k in SCRATCH[:4])
    chosen_cat, mixed_cat, start, diags, gain, shift, partial, part = (refs[k] for k in SCRATCH[4:12])
    rs_x, rs_far, rs_out, rs_z, heff, corr, xnow, hnow, mixed, mixed_in, tiles = (refs[k] for k in SCRATCH[12:23])
    load_sem, ex_send, ex_recv, rsx_send, rsx_recv, rsf_send, rsf_recv = (refs[k] for k in SCRATCH[23:30])
    rsz_send, rsz_recv, agz_send, agx_send, agf_send, ag_recv, side_send = (refs[k] for k in SCRATCH[30:37])
    side_recv, mix_send, mix_recv, sum_send, sum_recv, wide_tiles, wide_send, wide_recv = (
        refs[k] for k in SCRATCH[37:45]
    )
    local_tile, turn_cat, quad, psi, diag = (refs[k] for k in SCRATCH[45:])
    N = psi.shape[0]
    Y = S // 2
    w = N // (X * Z)
    block = N // X
    ops = lax.axis_index("ops")
    sec = lax.axis_index("sec")
    x, z = ops // Z, ops % Z
    y, core = sec // 2, sec % 2
    partner = y * 2 + (1 - core)
    outer = (sec + 2 * core - 1 + S) % S
    far = [d for d in reversed(near_first(Z)) if min(d, Z - d) >= FAR]
    near = [d for d in near_first(Z) if d not in far]
    around = near_first(X)

    def at(xd, zd):
        return {"ops": xd * Z + zd, "sec": sec}

    def off(dx, dz):
        return at((x + dx) % X, (z + dz) % Z)

    sides = ({"ops": ops, "sec": partner}, {"ops": ops, "sec": outer})
    xcore = [{"ops": ((x + d) % X) * Z + z, "sec": y * 2 + c} for d in range(X) for c in (core, 1 - core)][1:]
    groups = (
        (x * 2 + core, xcore),
        (z, [off(0, d) for d in range(1, Z)]),
        (y, [{"ops": ops, "sec": ((y + d) % Y) * 2 + core} for d in range(1, Y)]),
    )

    plane = [(dx, dz) for dz in reversed([0] + near_first(Z)) for dx in reversed([0] + around) if dx or dz]
    wide_groups = (
        (ops, [off(dx, dz) for dx, dz in plane]),
        (
            sec,
            [
                {"ops": ops, "sec": ((y + d) % Y) * 2 + c}
                for d in reversed([0] + near_first(Y))
                for c in ((1 - core, core) if d else (1 - core,))
            ],
        ),
    )

    barrier = pltpu.get_barrier_semaphore()
    peers = [device for _, members in groups for device in members] + [sides[1]]
    peers += [off(dx, dz) for dx in around for dz in far]
    for device in peers:
        pl.semaphore_signal(barrier, inc=1, device_id=device, device_id_type=MESH)

    early = [
        pltpu.make_async_copy(psi_hbm, psi, load_sem.at[2]),
        pltpu.make_async_copy(diag_hbm, diag, load_sem.at[3]),
    ]
    loads = [
        pltpu.make_async_copy(left_hbm, left, load_sem.at[0]),
        pltpu.make_async_copy(right_hbm, right, load_sem.at[1]),
    ]
    for load in early + loads:
        load.start()

    size = states[0]
    rows_at = lax.broadcasted_iota(jnp.int32, (N, N), 0)
    cols_at = lax.broadcasted_iota(jnp.int32, (N, N), 1)
    live = ((rows_at < size) & (cols_at < size)).astype(F32)
    for load in early:
        load.wait()
    start[0] = psi[...].astype(F32) * live
    diags[0] = diag[...].astype(F32)

    pl.semaphore_wait(barrier, len(peers))

    def send(src, dst, send_sem, recv_sem, device):
        copy = pltpu.make_async_remote_copy(
            src_ref=src,
            dst_ref=dst,
            send_sem=send_sem,
            recv_sem=recv_sem,
            device_id=device,
            device_id_type=MESH,
        )
        copy.start()

    def settle(like, sem):
        pltpu.make_async_copy(like, like, sem).wait()

    for g in range(X):
        rows = pl.ds(g * block, block)
        send(start.at[0, rows], start.at[2, rows], ex_send.at[0], ex_recv.at[g], sides[1])
    send(start.at[0], start.at[1], ex_send.at[1], ex_recv.at[X], sides[0])

    for load in loads:
        load.wait()
    for p in range(2):
        high, low = split(left[p])
        for q, piece in enumerate((high, high, low)):
            left_cat[p, :, q * N : (q + 1) * N] = piece
        high, low = split(right[p].T)
        for q, piece in enumerate((high, low, high)):
            right_cat[(3 * p + q) * N : (3 * p + q + 1) * N] = piece

    picks = []
    for p in range(2):
        source = couple[p]
        row = []
        for target in (sec, partner, outer):
            row.append(jnp.where((source == target) & (source >= 0), 1.0, 0.0).astype(F32))
        picks.append(row)

    def choose_inner(own, other):
        for p in range(2):
            partial[p] = picks[p][0] * own + picks[p][1] * other

    def choose_outer(rows_from, value):
        for p in range(2):
            high, low = split(partial[p, pl.ds(rows_from, block)] + picks[p][2] * value)
            for q, piece in enumerate((high, low, high)):
                chosen_cat[p, pl.ds(q * N + rows_from, block)] = piece

    half = X // 2
    upper = x // half

    def apply_half(i, which):
        rows = pl.ds(pl.multiple_of(which * (N // 2), N // 2), N // 2)
        for p in range(2):
            value = dot(left_cat[p, rows], chosen_cat[p])
            mixed[i, p, rows] = value
            high, low = split(value)
            for q, piece in enumerate((high, high, low)):
                mixed_cat[:, (3 * p + q) * N : (3 * p + q + 1) * N] = piece
        part[i, rows] = dot(mixed_cat[...], right_cat[...])

    def slice_of(index):
        return pl.ds(pl.multiple_of(index * w, w), w)

    def scatter_to(i, xd):
        for f, dz in enumerate(far):
            zd = (z + dz) % Z
            send(part.at[i, slice_of(xd * Z + zd)], rs_far.at[i, x, f], rsf_send.at[i], rsf_recv.at[i], at(xd, zd))

    def scatter_along(i, xd):
        for k, dz in reversed(list(enumerate([0] + near))):
            src = part.at[i, slice_of(xd * Z + (z + dz) % Z)]
            send(src, rs_x.at[i, x, k], rsx_send.at[i], rsx_recv.at[i, k], at(xd, z))

    def apply(i, scatter):
        apply_half(i, 1 - upper)
        away = [(1 - upper) * half + j for j in range(half)]
        beside = [x + 1 - 2 * (x % 2)] if half == 2 else []
        if scatter:
            for xd in away:
                scatter_to(i, xd)
                scatter_along(i, xd)
        apply_half(i, upper)
        if scatter:
            for xd in beside + [x]:
                scatter_to(i, xd)
            for xd in beside:
                scatter_along(i, xd)
        send(mixed.at[i], mixed_in.at[i], mix_send.at[i], mix_recv.at[i], sides[0])

    def summed_over_x(i, k, dz):
        settle(rs_x.at[i, pl.ds(0, X - 1), 0], rsx_recv.at[i, k])
        total = part[i, slice_of(x * Z + (z + dz) % Z)]
        for dx in range(1, X):
            total = total + rs_x[i, (x + dx) % X, k]
        return total

    def scatter_middle(i):
        for k, dz in reversed(list(enumerate([0] + near))):
            rs_out[i, k] = summed_over_x(i, k, dz)
            if k > 0:
                send(rs_out.at[i, k], rs_z.at[i, k], rsz_send.at[i], rsz_recv.at[i], off(0, dz))

    def scatter_end(i):
        total = rs_out[i, 0]
        if near:
            settle(rs_z.at[i, pl.ds(0, len(near))], rsz_recv.at[i])
            for k in range(1, len(near) + 1):
                total = total + rs_z[i, k]
        if far:
            settle(rs_far.at[i], rsf_recv.at[i])
            for xs in range(X):
                for f in range(len(far)):
                    total = total + rs_far[i, xs, f]
        rows = lax.broadcasted_iota(jnp.int32, (w, N), 0) + ops * w
        cols = lax.broadcasted_iota(jnp.int32, (w, N), 1)
        mask = ((rows < size) & (cols < size)).astype(F32)
        heff[i, 0, slice_of(ops)] = total * mask

    def to_sides(i, dx, index):
        src = heff.at[i, 0, slice_of(index)]
        send(src, heff.at[i, 2, slice_of(index)], side_send.at[i, 1], side_recv.at[i, 1 + dx], sides[1])
        if not BULK:
            send(src, heff.at[i, 1, slice_of(index)], side_send.at[i, 0], side_recv.at[i, 0], sides[0])

    def gather_start(i):
        src = heff.at[i, 0, slice_of(ops)]
        for dz in far:
            for dx in list(reversed(around)) + [0]:
                send(src, src, agf_send.at[i], ag_recv.at[i, ops], off(dx, dz))
        for dz in reversed(near):
            send(src, src, agz_send.at[i], ag_recv.at[i, ops], off(0, dz))
        for dx in reversed(around):
            send(src, src, agx_send.at[i], ag_recv.at[i, ops], off(dx, 0))
        to_sides(i, 0, ops)

    def gather_along_x(i):
        for dz in near:
            index = x * Z + (z + dz) % Z
            src = heff.at[i, 0, slice_of(index)]
            settle(src, ag_recv.at[i, index])
            for dx in reversed(around):
                send(src, src, agx_send.at[i], ag_recv.at[i, index], off(dx, 0))
            to_sides(i, 0, index)

    def gather_end(i):
        rest = [(dx, 0) for dx in around] + [(0, dz) for dz in reversed(far)]
        rest += [(dx, dz) for dz in near for dx in around]
        rest += [(dx, dz) for dz in reversed(far) for dx in around]
        for dx, dz in rest:
            index = ((x + dx) % X) * Z + (z + dz) % Z
            settle(heff.at[i, 0, slice_of(index)], ag_recv.at[i, index])
            to_sides(i, dx, index)
        if BULK:
            send(heff.at[i, 0], heff.at[i, 1], side_send.at[i, 0], side_recv.at[i, 0], sides[0])

    def reduction_sends_done(i):
        for _ in range(X - 1):
            settle(rs_x.at[i, 0, pl.ds(0, 1 + len(near))], rsx_send.at[i])
            settle(rs_x.at[i, 0, pl.ds(0, 1 + len(near))], agx_send.at[i])
        if far:
            settle(rs_far.at[i], rsf_send.at[i])
            settle(rs_far.at[i], agf_send.at[i])
        if near:
            settle(rs_z.at[i, pl.ds(0, len(near))], rsz_send.at[i])
            settle(rs_z.at[i, pl.ds(0, len(near))], agz_send.at[i])
        for j in range(2):
            settle(heff.at[i, 0], side_send.at[i, j])

    def sum_start(i, stage, tile):
        mine, members = groups[stage]
        slot = tiles.at[i, stage, mine]
        slot[...] = tile
        for device in members:
            send(slot, slot, sum_send.at[i, stage], sum_recv.at[i, stage], device)

    def sum_end(i, stage):
        others = len(groups[stage][1])
        settle(tiles.at[i, stage, pl.ds(0, others)], sum_recv.at[i, stage])
        total = tiles[i, stage, 0]
        for slot in range(1, others + 1):
            total = total + tiles[i, stage, slot]
        return total

    def sums_done(i):
        for stage in range(3):
            others = len(groups[stage][1])
            settle(tiles.at[i, stage, pl.ds(0, others)], sum_send.at[i, stage])

    def wide_start(stage, row):
        mine, members = wide_groups[stage]
        slot = wide_tiles.at[stage, mine]
        slot[...] = row
        for device in members:
            send(slot, slot, wide_send.at[stage], wide_recv.at[stage], device)

    def wide_end(stage):
        others = len(wide_groups[stage][1])
        settle(wide_tiles.at[stage, pl.ds(0, others)], wide_recv.at[stage])
        totals = [wide_tiles[stage, slot] for slot in range(others + 1)]
        while len(totals) > 1:
            totals = [sum(totals[j : j + 2]) for j in range(0, len(totals), 2)]
        return totals[0]

    def wide_done(stage):
        others = len(wide_groups[stage][1])
        settle(wide_tiles.at[stage, pl.ds(0, others)], wide_send.at[stage])

    lane = lax.broadcasted_iota(jnp.int32, (8, 128), 1)
    sublane = lax.broadcasted_iota(jnp.int32, (8, 128), 0)

    def packed(tile):
        columns = jnp.sum(tile, axis=1, keepdims=True)
        return jnp.sum(jnp.where(lane == sublane, columns, 0.0), axis=0, keepdims=True)

    def unpacked(row):
        return jnp.where(lane == sublane, row, 0.0)

    share = 1.0 / (X * Z)

    def reduce(i, tile):
        sum_start(i, 0, tile)
        scatter_middle(i)
        sum_start(i, 1, sum_end(i, 0))
        scatter_end(i)
        gather_start(i)
        sum_start(i, 2, sum_end(i, 1))
        gather_along_x(i)
        gather_end(i)

    def correct(i, own, hown):
        c = gain[0] * heff[i, 0] - shift[0]
        corr[i, 0] = c
        settle(heff.at[i, 1], side_recv.at[i, 0])
        corr[i, 1] = gain[1] * heff[i, 1] - shift[1]
        choose_inner(corr[i, 0], corr[i, 1])
        rest = [value * share for value in (own * c, c * c, c * hown, own * own, own * hown)]
        local_tile[...] = tile_of([jnp.zeros_like(own)] * 2 + rest)
        for dx in [0] + around:
            rows_from = pl.multiple_of(((x + dx) % X) * block, block)
            rows = pl.ds(rows_from, block)
            settle(heff.at[i, 2, rows], side_recv.at[i, 1 + dx])
            value = gain[2, rows] * heff[i, 2, rows] - shift[2, rows]
            corr[i, 2, rows] = value
            choose_outer(rows_from, value)

    settle(start.at[1], ex_recv.at[X])
    choose_inner(start[0], start[1])
    for g in range(X):
        rows = pl.ds(g * block, block)
        settle(start.at[2, rows], ex_recv.at[g])
        choose_outer(g * block, start[2, rows])
    apply(0, True)
    for j in range(2):
        send(diags.at[0], diags.at[1 + j], ex_send.at[2 + j], ex_recv.at[X + 1 + j], sides[j])
    own, term = start[0], part[0]
    reduce(0, tile_of([own * own * share, own * term]))
    squares, energy = scalars_of(sum_end(0, 2), 2)
    factor = lax.rsqrt(squares + TINY)
    theta = energy * factor * factor
    for j in range(2):
        settle(diags.at[1 + j], ex_recv.at[X + 1 + j])
    for b in range(3):
        inverse = 1.0 / (jnp.abs(diags[b] - theta) + 1.0)
        gain[b] = factor * inverse
        shift[b] = (theta * factor) * start[b] * inverse
    correct(0, factor * start[0], factor * heff[0, 0])

    def products(term, own, c):
        return local_tile[...] + tile_of([own * term, c * term])

    apply(1, True)
    reduce(1, products(part[1], factor * start[0], corr[0, 0]))
    alpha, beta, theta = turn(sum_end(1, 2), theta)
    alpha = alpha * factor
    for b in range(3):
        xb = alpha * start[b] + beta * corr[0, b]
        inverse = 1.0 / (jnp.abs(diags[b] - theta) + 1.0)
        xnow[b] = xb
        gain[b] = beta * inverse
        shift[b] = (theta * xb - alpha * heff[0, b]) * inverse
    hnow[...] = alpha * heff[0, 0] + beta * heff[1, 0]
    correct(1, xnow[0], hnow[...])

    apply(2, False)
    wide_start(0, packed(products(part[2], xnow[0], corr[1, 0])))
    keep = jnp.where(labels[0] == sec, 1.0, 0.0).astype(F32)
    swap = 1.0 - keep
    for i in range(3):
        settle(mixed_in.at[i], mix_recv.at[i])
        settle(mixed_in.at[i], mix_send.at[i])
    root = 1.0 / jnp.sqrt(jnp.float32(N))
    sources = (xnow, corr.at[1])
    for q, source in enumerate(sources):
        value = (keep * source[0] + swap * source[1]) * root
        turn_cat[q, 0], turn_cat[q, 1] = split(value.T)

    def turned_by(q, value):
        high, low = value
        return dot(turn_cat[q, 0], high) + (dot(turn_cat[q, 0], low) + dot(turn_cat[q, 1], high))

    def quadratic(p):
        first = alpha * mixed[0, p] + beta * mixed[1, p]
        other = alpha * mixed_in[0, p] + beta * mixed_in[1, p]
        first = split(keep * first + swap * other)
        second = split(keep * mixed[2, p] + swap * mixed_in[2, p])
        quad[p, 0] = turned_by(0, first)
        quad[p, 1] = turned_by(0, second) + turned_by(1, first)
        quad[p, 2] = turned_by(1, second)

    quadratic(0)
    wide_start(1, wide_end(0))
    quadratic(1)
    for i in range(2):
        reduction_sends_done(i)
        sums_done(i)
    for j in range(2):
        settle(start.at[0], ex_send.at[j])
        settle(diags.at[0], ex_send.at[2 + j])
    wide_done(0)
    alpha, beta, theta = turn(unpacked(wide_end(1)), theta)
    scale = jnp.sqrt(jnp.float32(S * N * N))
    alpha, beta = alpha * scale, beta * scale
    wave[...] = alpha * xnow[0] + beta * corr[1, 0]
    aa, ab, bb = alpha * alpha, alpha * beta, beta * beta
    for p in range(2):
        rotated[p] = (aa * quad[p, 0] + ab * quad[p, 1]) + bb * quad[p, 2]
    wide_done(1)


def handed_on(wave, rotated, wave_out, rotated_out, sem):
    copies = [
        pltpu.make_async_copy(rotated, rotated_out, sem.at[0]),
        pltpu.make_async_copy(wave, wave_out, sem.at[1]),
    ]
    for copy in copies:
        copy.start()
    for copy in copies:
        copy.wait()


def local(X, sector_states, psi_guess, precond_diag, left_ops, right_ops, couple, new_sector):
    N = psi_guess.shape[1]
    S = lax.axis_size("sec")
    Z = lax.axis_size("ops") // X
    pairs = left_ops.shape[0]
    w = N // (X * Z)
    G = max(2 * X, Z, S // 2)
    F = max(1, sum(min(d, Z - d) >= FAR for d in range(1, Z)))
    dma = pltpu.SemaphoreType.DMA
    smem = pl.BlockSpec(memory_space=pltpu.SMEM)
    vmem = pl.BlockSpec(memory_space=pltpu.VMEM)
    hbm = pl.BlockSpec(memory_space=pl.ANY)
    shapes = {
        "left": (2, N, N),
        "right": (2, N, N),
        "left_cat": (2, N, 3 * N),
        "right_cat": (6 * N, N),
        "chosen_cat": (2, 3 * N, N),
        "mixed_cat": (N // 2, 6 * N),
        "start": (3, N, N),
        "diags": (3, N, N),
        "gain": (3, N, N),
        "shift": (3, N, N),
        "partial": (2, N, N),
        "part": (3, N, N),
        "rs_x": (2, X, Z, w, N),
        "rs_far": (2, X, F, w, N),
        "rs_out": (2, Z, w, N),
        "rs_z": (2, Z, w, N),
        "heff": (2, 3, N, N),
        "corr": (2, 3, N, N),
        "xnow": (3, N, N),
        "hnow": (N, N),
        "mixed": (3, 2, N, N),
        "mixed_in": (3, 2, N, N),
        "tiles": (2, 3, G, 8, 128),
        "local_tile": (8, 128),
        "turn_cat": (2, 2, N, N),
        "quad": (2, 3, N, N),
        "psi": (N, N),
        "diag": (N, N),
        "wide_tiles": (2, max(X * Z, S), 1, 128),
    }
    sems = {
        "load_sem": (4,),
        "ex_send": (4,),
        "ex_recv": (X + 3,),
        "rsx_recv": (2, Z),
        "ag_recv": (2, X * Z),
        "side_send": (2, 2),
        "side_recv": (2, 1 + X),
        "mix_send": (3,),
        "mix_recv": (3,),
        "sum_send": (3, 3),
        "sum_recv": (3, 3),
    }
    scratch = []
    for name in SCRATCH:
        if name in shapes:
            scratch.append(pltpu.VMEM(shapes[name], BF16 if name.endswith("_cat") or name in ("psi", "diag") else F32))
        else:
            scratch.append(dma(sems.get(name, (2,))))
    outs = (
        jax.ShapeDtypeStruct((N, N), F32),
        jax.ShapeDtypeStruct((pairs, N, N), F32),
    )
    wave, rotated = pl.pallas_call(
        functools.partial(kernel, X, Z, S),
        out_shape=(pltpu.VMEM((N, N), F32), pltpu.VMEM((pairs, N, N), F32)),
        in_specs=[smem, smem, smem, hbm, hbm, hbm, hbm],
        out_specs=(vmem, vmem),
        scratch_shapes=scratch,
        compiler_params=pltpu.CompilerParams(collective_id=0, has_side_effects=True),
    )(
        sector_states,
        couple[:, 0],
        new_sector,
        psi_guess[0],
        precond_diag[0],
        left_ops[:, 0],
        right_ops[:, 0],
    )
    if HAND_ON:
        wave, rotated = pl.pallas_call(
            handed_on,
            out_shape=outs,
            in_specs=[vmem, vmem],
            out_specs=(hbm, hbm),
            scratch_shapes=[dma((2,))],
        )(*(pltpu.with_memory_space_constraint(value, pltpu.VMEM) for value in (wave, rotated)))
    return wave[None], rotated[:, None]


def solution(mesh):
    count = mesh.shape["ops"]
    X = 4 if count == 32 else 2
    in_specs = (
        P("sec"),
        P("sec", None, None),
        P("sec", None, None),
        P("ops", "sec", None, None),
        P("ops", "sec", None, None),
        P("ops", "sec"),
        P("sec"),
    )
    out_specs = (P("sec", None, None), P("ops", "sec", None, None))
    return jax.shard_map(
        functools.partial(local, X), mesh=mesh, in_specs=in_specs, out_specs=out_specs, check_vma=False
    )
```
